32 devices in a mesh: task: 4 (over z), shard: 2 (over y), rep: 4 (over x, core).
Axes of the slice: x: 2, y: 2, z: 4, core: 2. Of those that a mesh axis runs over, the one named last changes fastest.
Arguments:
- deltas: bfloat16 [8, 32, 16, 8192], P('task', None, None, ('shard', 'rep')), may hold values from -4 to 4
- base: bfloat16 [32, 16, 2, 4096], P(('task', 'shard'), None, None, 'rep'), may hold values from -60 to 60
- sel_index: int32 [8, 8], replicated, may hold values from 0 to 31, as said below
- sel_count: int32 [8], replicated, may hold values from 1 to 8
- scale_num: int32 [8], replicated, may hold values from 1 to 12
Outputs:
- merged: bfloat16 [32, 16, 8192], P(('task', 'shard'))
The draws below stay inside these ranges and needn't reach their ends.
Inputs may be any that keep to these rules, and one draw needn't show every extreme that they name: `sel_index`: for task i the first sel_count[i] entries are distinct and ascending; at most 1 of them lie in any aligned group of 4 blocks, and in every draw some group holds 1 selected blocks of every task, and some task selects 1 block in every group. Later entries are block numbers that are not selected.
All inputs are finite; a program needn't handle non-finite values.
Results may differ from the reference program's by a relative error of at most 0.00045.
Values may be sent and summed in bfloat16 or wider, within the bound.
A program may use at most 64 MiB of HBM per device.

```python
import jax
import jax.numpy as jnp
from jax import lax

D = 8192
LAYERS = 4
BR = 16
OB = 4
CAP = 1
OWNERS = 8
NB_ALL = 32
KMAX = 8
TASKS = 8
N_SHARD = 2


def pick_blocks(key):
    inner = jax.random.fold_in(key, 11)
    keys = jax.random.split(inner, 5)
    counts = jax.random.randint(keys[0], (TASKS, OWNERS), 0, CAP + 1)
    common = jax.random.randint(keys[1], (), 0, OWNERS)
    single = jax.random.randint(keys[2], (TASKS,), 0, OWNERS)
    full_task = jax.random.randint(keys[4], (), 0, TASKS)
    owner_ids = jnp.arange(OWNERS, dtype=jnp.int32)
    task_ids = jnp.arange(TASKS, dtype=jnp.int32)
    filled = (owner_ids[None, :] == common) | (owner_ids[None, :] == single[:, None]) | (task_ids[:, None] == full_task)
    counts = jnp.where(filled, CAP, counts)
    scores = jax.random.randint(keys[3], (TASKS, OWNERS, OB), 0, 1 << 20) * OB + jnp.arange(OB, dtype=jnp.int32)
    order = jnp.argsort(scores, axis=-1)
    ranks = jnp.argsort(order, axis=-1)
    chosen = (ranks < counts[:, :, None]).reshape(TASKS, NB_ALL)
    blocks = jnp.arange(NB_ALL, dtype=jnp.int32)
    sort_key = jnp.where(chosen, blocks[None, :], NB_ALL + blocks[None, :])
    listed = jnp.argsort(sort_key, axis=1)[:, :KMAX].astype(jnp.int32)
    total = jnp.sum(chosen.astype(jnp.int32), axis=1).astype(jnp.int32)
    return (listed, total)


def draw_sel_index(key, part):
    return pick_blocks(key)[0]


def draw_sel_count(key, part):
    return pick_blocks(key)[1]


def base_values(key):
    keys = jax.random.split(jax.random.fold_in(key, 5), 2)
    group_cols = D // N_SHARD
    shape = (NB_ALL, BR, N_SHARD, group_cols)
    block_rise = 0.6 * jnp.exp(jnp.log(3.0) * jnp.arange(NB_ALL, dtype=jnp.float32) / max(NB_ALL - 1, 1))
    col_rise = 0.6 * jnp.exp(jnp.log(3.0) * jnp.arange(group_cols, dtype=jnp.float32) / max(group_cols - 1, 1))
    noise = jnp.clip(jax.random.normal(keys[0], shape, jnp.float32), -6.0, 6.0)
    row_scale = jnp.exp(jax.random.uniform(keys[1], (NB_ALL, BR), jnp.float32, jnp.log(0.5), jnp.log(2.0)))
    values = noise * block_rise[:, None, None, None] * row_scale[:, :, None, None]
    values = values * col_rise[None, None, None, :]
    return values


def draw_base(key, part):
    return base_values(key).astype(jnp.bfloat16)


def draw_deltas(key, part):
    keys = jax.random.split(jax.random.fold_in(key, 23), 2)
    shaped = base_values(key).reshape(NB_ALL, BR, D)
    noise = 0.45 * jnp.clip(jax.random.normal(keys[0], (TASKS, NB_ALL, BR, D), jnp.float32), -6.0, 6.0)
    shared = 0.3 * jnp.clip(jax.random.normal(keys[1], (NB_ALL, BR, D), jnp.float32), -6.0, 6.0)
    tie = 0.04
    values = noise + shared[None] + tie * shaped[None]
    return jnp.clip(values, -4.0, 4.0).astype(jnp.bfloat16)


def place_ends(drawn, key, least, top_value):
    extent = drawn.shape
    spot = [jax.random.randint(jax.random.fold_in(key, axis), (), 0, extent[axis]) for axis in range(len(extent))]
    drawn = drawn.at[tuple(spot)].set(least)
    longest = extent.index(max(extent))
    spot[longest] = (spot[longest] + 1) % extent[longest]
    return drawn.at[tuple(spot)].set(top_value)


def setup_inputs(seed: int = 0) -> dict:
    seeds = jax.random.split(jax.random.key(seed), 6)
    return {
        "deltas": draw_deltas(jax.random.fold_in(seeds[5], 71), 0),
        "base": draw_base(jax.random.fold_in(seeds[5], 71), 0),
        "sel_index": draw_sel_index(jax.random.fold_in(seeds[5], 71), 0),
        "sel_count": draw_sel_count(jax.random.fold_in(seeds[5], 71), 0),
        "scale_num": place_ends(jax.random.randint(seeds[4], (TASKS,), 1, 13), jax.random.fold_in(seeds[4], 1), 1, 12).astype(jnp.int32),
    }


denominator = 8.0
epsilon = 1e-06

def reference(deltas, base, sel_index, sel_count, scale_num):
    entries = jnp.arange(KMAX, dtype=jnp.int32)
    valid = entries[None, :] < sel_count[:, None]
    blocks = jnp.arange(NB_ALL, dtype=jnp.int32)
    hits = (sel_index[:, :, None] == blocks[None, None, :]) & valid[:, :, None]
    picked = lax.optimization_barrier(jnp.sum(hits.astype(jnp.float32), axis=1))
    weight = picked * (scale_num.astype(jnp.float32) / denominator)[:, None]

    def accumulate(total, item):
        delta, factor = item
        return (total + factor[:, None, None] * delta.astype(jnp.float32), None)
    combined, _ = lax.scan(accumulate, jnp.zeros((NB_ALL, BR, D), jnp.float32), (deltas, weight))
    base_full = base.reshape(NB_ALL, BR, D).astype(jnp.float32)
    merged_raw = base_full + combined
    span = NB_ALL // LAYERS
    base_sq = lax.optimization_barrier(jnp.sum(lax.optimization_barrier(jnp.sum(base_full * base_full, axis=(1, 2))).reshape(LAYERS, span), axis=1))
    merged_sq = lax.optimization_barrier(jnp.sum(lax.optimization_barrier(jnp.sum(merged_raw * merged_raw, axis=(1, 2))).reshape(LAYERS, span), axis=1))
    ratio = jnp.sqrt((base_sq + epsilon) / (merged_sq + epsilon))
    per_block = ratio[blocks // span]
    return (merged_raw * per_block[:, None, None]).astype(jnp.bfloat16)
```

```python
import functools

import jax
import jax.numpy as jnp
from jax import lax
from jax.experimental import pallas as pl
from jax.experimental.pallas import tpu as pltpu
from jax.sharding import PartitionSpec as P

LAYERS = 4
LANES = 128
MESH = pl.DeviceIdType.MESH

denominator = 8.0
epsilon = 1e-06


def offset_peers(n_task, n_shard, n_rep, layer_tasks):
    owners = [(a, b) for a in range(n_task) for b in range(n_shard)][1:]
    group = [(a, b, c) for a in range(layer_tasks) for b in range(n_shard) for c in range(n_rep)][1:]
    return owners, group


def kernel(
    dims, index_ref, count_ref, scale_ref, deltas_ref, base_ref, out_ref,
    held, base_held, outgoing, incoming, raw, stat_mine, stat_in,
    load_sems, base_sem, send_sems, recv_sems, stat_send, stat_recv, col_send, col_recv,
):
    n_task, n_shard, n_rep, layer_tasks = dims
    task_dev, nb_all, rows, width = deltas_ref.shape
    groups, own_blocks = raw.shape[:2]
    group_cols = out_ref.shape[2] // groups
    kmax = index_ref.shape[1]
    owner_offsets, stat_offsets = offset_peers(n_task, n_shard, n_rep, layer_tasks)

    my_task = lax.axis_index("task")
    my_shard = lax.axis_index("shard")
    my_rep = lax.axis_index("rep")

    loads = []
    for a in range(task_dev):
        copy = pltpu.make_async_copy(deltas_ref.at[a], held.at[a], load_sems.at[a])
        copy.start()
        loads.append(copy)
    base_copy = pltpu.make_async_copy(base_ref, base_held, base_sem)
    base_copy.start()

    def owner_at(off, sign=1):
        t = lax.rem(my_task + sign * off[0] + n_task, n_task)
        s = lax.rem(my_shard + sign * off[1] + n_shard, n_shard)
        return t, s

    layer_first = (my_task // layer_tasks) * layer_tasks

    def stat_at(off):
        t = layer_first + lax.rem(my_task - layer_first + off[0], layer_tasks)
        s = lax.rem(my_shard + off[1], n_shard)
        r = lax.rem(my_rep + off[2], n_rep)
        return t, s, r

    barrier = pltpu.get_barrier_semaphore()
    for off in owner_offsets:
        t, s = owner_at(off)
        pl.semaphore_signal(barrier, inc=1, device_id=(t, s, my_rep), device_id_type=MESH)
    extra = [o for o in stat_offsets if o[2] != 0 or (o[0] != 0 and n_task % layer_tasks)]
    for off in extra:
        pl.semaphore_signal(barrier, inc=1, device_id=stat_at(off), device_id_type=MESH)

    def block_for(task, owner):
        count = count_ref[task]

        def step(k, carry):
            block, live = carry
            entry = index_ref[task, k]
            hit = (k < count) & (entry // own_blocks == owner)
            return jnp.where(hit, entry, block), jnp.where(hit, 1, live)

        start = (owner * own_blocks, jnp.int32(0))
        return lax.fori_loop(0, kmax, step, start, unroll=kmax <= 8)

    chosen = {}
    for d, off in enumerate([(0, 0)] + owner_offsets):
        t, s = owner_at(off)
        for a in range(task_dev):
            chosen[d, a] = block_for(my_task * task_dev + a, t * n_shard + s)[0]

    for copy in loads:
        copy.wait()

    for d, off in enumerate(owner_offsets):
        for a in range(task_dev):
            outgoing[d, a] = held[a, chosen[d + 1, a]]

    pl.semaphore_wait(barrier, len(owner_offsets) + len(extra))

    sends = []
    for d, off in enumerate(owner_offsets):
        t, s = owner_at(off)
        copy = pltpu.make_async_remote_copy(
            src_ref=outgoing.at[d], dst_ref=incoming.at[d],
            send_sem=send_sems.at[d], recv_sem=recv_sems.at[d],
            device_id=(t, s, my_rep), device_id_type=MESH,
        )
        copy.start()
        sends.append(copy)

    def fold(values):
        total = values[:, 0:LANES]
        for c in range(LANES, values.shape[1], LANES):
            total = total + values[:, c:c + LANES]
        return total

    base_copy.wait()
    base_sum = jnp.zeros((rows, LANES), jnp.float32)
    for g in range(groups):
        for j in range(own_blocks):
            wide = base_held[j, g].astype(jnp.float32)
            raw[g, j] = wide
            base_sum = base_sum + fold(wide * wide)
    stat_mine[0] = base_sum

    my_owner = my_task * n_shard + my_shard

    def add_in(off, pieces):
        t, s = owner_at(off, -1)
        weights = []
        for a in range(task_dev):
            task = t * task_dev + a
            block, live = block_for(task, my_owner)
            factor = scale_ref[task].astype(jnp.float32) / denominator
            factor = jnp.where(live == 1, factor, 0.0)
            local = block - my_owner * own_blocks
            weights.append([jnp.where(local == j, factor, 0.0) for j in range(own_blocks)])
        pieces = [p.astype(jnp.float32) for p in pieces()]
        for j in range(own_blocks):
            total = raw[s, j]
            for a in range(task_dev):
                total = total + weights[a][j] * pieces[a]
            raw[s, j] = total

    add_in((0, 0), lambda: [held[a, chosen[0, a]] for a in range(task_dev)])
    for d, off in enumerate(owner_offsets):
        def pieces(d=d):
            sends[d].wait_recv()
            return [incoming[d, a] for a in range(task_dev)]
        add_in(off, pieces)

    merged_sum = jnp.zeros((rows, LANES), jnp.float32)
    for g in range(groups):
        for j in range(own_blocks):
            value = raw[g, j]
            merged_sum = merged_sum + fold(value * value)
    stat_mine[1] = merged_sum

    stats = []
    for e, off in enumerate(stat_offsets):
        copy = pltpu.make_async_remote_copy(
            src_ref=stat_mine, dst_ref=stat_in.at[e],
            send_sem=stat_send.at[e], recv_sem=stat_recv.at[e],
            device_id=stat_at(off), device_id_type=MESH,
        )
        copy.start()
        stats.append(copy)
    base_total, merged_total = base_sum, merged_sum
    for e in range(len(stat_offsets)):
        stats[e].wait_recv()
        base_total = base_total + stat_in[e, 0]
        merged_total = merged_total + stat_in[e, 1]
    base_total = jnp.sum(base_total, axis=(0, 1), keepdims=True)
    merged_total = jnp.sum(merged_total, axis=(0, 1), keepdims=True)
    ratio = jnp.sqrt((base_total + epsilon) / (merged_total + epsilon))

    cols = []
    for g in range(groups):
        col = pl.multiple_of(g * group_cols + my_rep * width, width)
        for j in range(own_blocks):
            out_ref[j, :, pl.ds(col, width)] = (raw[g, j] * ratio).astype(jnp.bfloat16)
        part = out_ref.at[:, :, pl.ds(col, width)]
        for c in range(1, n_rep):
            copy = pltpu.make_async_remote_copy(
                src_ref=part, dst_ref=part,
                send_sem=col_send.at[g, c - 1], recv_sem=col_recv.at[g, c - 1],
                device_id=(my_task, my_shard, lax.rem(my_rep + c, n_rep)), device_id_type=MESH,
            )
            copy.start()
            cols.append(copy)
    for copy in cols:
        copy.wait_recv()
    for copy in sends + stats + cols:
        copy.wait_send()


def solution(mesh):
    n_task, n_shard, n_rep = mesh.shape["task"], mesh.shape["shard"], mesh.shape["rep"]

    def shards(deltas, base, sel_index, sel_count, scale_num):
        task_dev, nb_all, rows, width = deltas.shape
        own_blocks, _, groups, _ = base.shape
        layer_tasks = nb_all // LAYERS // own_blocks // n_shard
        dims = (n_task, n_shard, n_rep, layer_tasks)
        peers, group = offset_peers(*dims)
        smem = pl.BlockSpec(memory_space=pltpu.SMEM)
        hbm = pl.BlockSpec(memory_space=pl.ANY)
        base = jnp.transpose(base, (0, 2, 1, 3))
        return pl.pallas_call(
            functools.partial(kernel, dims),
            out_shape=jax.ShapeDtypeStruct((own_blocks, rows, groups * n_rep * width), jnp.bfloat16),
            in_specs=[smem, smem, smem, hbm, hbm],
            out_specs=pl.BlockSpec(memory_space=pltpu.VMEM),
            scratch_shapes=[
                pltpu.VMEM(deltas.shape, jnp.bfloat16),
                pltpu.VMEM(base.shape, jnp.bfloat16),
                pltpu.VMEM((len(peers), task_dev, rows, width), jnp.bfloat16),
                pltpu.VMEM((len(peers), task_dev, rows, width), jnp.bfloat16),
                pltpu.VMEM((groups, own_blocks, rows, width), jnp.float32),
                pltpu.VMEM((2, rows, LANES), jnp.float32),
                pltpu.VMEM((len(group), 2, rows, LANES), jnp.float32),
                pltpu.SemaphoreType.DMA((task_dev,)),
                pltpu.SemaphoreType.DMA,
                pltpu.SemaphoreType.DMA((len(peers),)),
                pltpu.SemaphoreType.DMA((len(peers),)),
                pltpu.SemaphoreType.DMA((len(group),)),
                pltpu.SemaphoreType.DMA((len(group),)),
                pltpu.SemaphoreType.DMA((groups, n_rep - 1)),
                pltpu.SemaphoreType.DMA((groups, n_rep - 1)),
            ],
            compiler_params=pltpu.CompilerParams(collective_id=0, has_side_effects=True),
        )(sel_index, sel_count, scale_num, deltas, base)

    placed = (
        P("task", None, None, ("shard", "rep")),
        P(("task", "shard"), None, None, "rep"),
        P(),
        P(),
        P(),
    )
    return jax.shard_map(
        shards,
        mesh=mesh,
        in_specs=placed,
        out_specs=P(("task", "shard"), None, None),
        check_vma=False,
    )
```

```python
import functools

import jax
import jax.numpy as jnp
from jax import lax
from jax.experimental import pallas as pl
from jax.experimental.pallas import tpu as pltpu
from jax.sharding import PartitionSpec as P

LAYERS = 4
LANES = 128
MESH = pl.DeviceIdType.MESH

denominator = 8.0
epsilon = 1e-06


def offset_peers(n_task, n_shard, n_rep, layer_tasks):
    order = sorted(range(n_task), key=lambda a: (-min(a, n_task - a), -a))
    owners = [(a, b) for a in order for b in range(n_shard) if a or b]
    group = [(a, b, c) for a in range(layer_tasks) for b in range(n_shard) for c in range(n_rep)][1:]
    return owners, group


def kernel(
    dims, index_hbm, count_hbm, scale_hbm, deltas_ref, base_ref, out_ref,
    index_ref, count_ref, scale_ref,
    held, base_held, outgoing, incoming, raw, mine, stat_mine, stat_in,
    table_sems, load_sems, base_sem, send_sems, recv_sems, stat_send, stat_recv,
    far_send, far_recv, near_send, near_recv, pass_send, pass_recv, keep_sems,
):
    n_task, n_shard, n_rep, layer_tasks = dims
    task_dev, nb_all, rows, width = deltas_ref.shape
    groups, own_blocks = raw.shape[:2]
    group_cols = out_ref.shape[2] // groups
    kmax = index_ref.shape[1]
    owner_offsets, stat_offsets = offset_peers(n_task, n_shard, n_rep, layer_tasks)

    my_task = lax.axis_index("task")
    my_shard = lax.axis_index("shard")
    my_rep = lax.axis_index("rep")

    tables = []
    for i, (src, dst) in enumerate(
        ((index_hbm, index_ref), (count_hbm, count_ref), (scale_hbm, scale_ref))
    ):
        copy = pltpu.make_async_copy(src, dst, table_sems.at[i])
        copy.start()
        tables.append(copy)
    loads = []
    for a in range(task_dev):
        copy = pltpu.make_async_copy(deltas_ref.at[a], held.at[a], load_sems.at[a])
        copy.start()
        loads.append(copy)
    base_copy = pltpu.make_async_copy(base_ref, base_held, base_sem)
    base_copy.start()

    def owner_at(off, sign=1):
        t = lax.rem(my_task + sign * off[0] + n_task, n_task)
        s = lax.rem(my_shard + sign * off[1] + n_shard, n_shard)
        return t, s

    layer_first = (my_task // layer_tasks) * layer_tasks

    def stat_at(off):
        t = layer_first + lax.rem(my_task - layer_first + off[0], layer_tasks)
        s = lax.rem(my_shard + off[1], n_shard)
        r = lax.rem(my_rep + off[2], n_rep)
        return t, s, r

    barrier = pltpu.get_barrier_semaphore()
    for off in owner_offsets:
        t, s = owner_at(off)
        pl.semaphore_signal(barrier, inc=1, device_id=(t, s, my_rep), device_id_type=MESH)
    extra = [o for o in stat_offsets if o[2] != 0]
    for off in extra:
        pl.semaphore_signal(barrier, inc=1, device_id=stat_at(off), device_id_type=MESH)

    for copy in tables:
        copy.wait()

    def block_for(task, owner):
        count = count_ref[task]

        def step(k, carry):
            block, live = carry
            entry = index_ref[task, k]
            hit = (k < count) & (entry // own_blocks == owner)
            return jnp.where(hit, entry, block), jnp.where(hit, 1, live)

        start = (owner * own_blocks, jnp.int32(0))
        return lax.fori_loop(0, kmax, step, start, unroll=kmax <= 8)

    chosen = {}
    for d, off in enumerate([(0, 0)] + owner_offsets):
        t, s = owner_at(off)
        for a in range(task_dev):
            chosen[d, a] = block_for(my_task * task_dev + a, t * n_shard + s)[0]

    for copy in loads:
        copy.wait()

    for d, off in enumerate(owner_offsets):
        for a in range(task_dev):
            outgoing[d, a] = held[a, chosen[d + 1, a]]

    pl.semaphore_wait(barrier, len(owner_offsets) + len(extra))

    sends = []
    for d, off in enumerate(owner_offsets):
        t, s = owner_at(off)
        copy = pltpu.make_async_remote_copy(
            src_ref=outgoing.at[d], dst_ref=incoming.at[d],
            send_sem=send_sems.at[d], recv_sem=recv_sems.at[d],
            device_id=(t, s, my_rep), device_id_type=MESH,
        )
        copy.start()
        sends.append(copy)

    def fold(values):
        total = values[:, 0:LANES]
        for c in range(LANES, values.shape[1], LANES):
            total = total + values[:, c:c + LANES]
        return total

    base_copy.wait()
    base_sum = jnp.zeros((rows, LANES), jnp.float32)
    for g in range(groups):
        for j in range(own_blocks):
            wide = base_held[j, :, g, :].astype(jnp.float32)
            raw[g, j] = wide
            base_sum = base_sum + fold(wide * wide)
    stat_mine[0] = base_sum

    my_owner = my_task * n_shard + my_shard

    def add_in(off, pieces):
        t, s = owner_at(off, -1)
        weights = []
        for a in range(task_dev):
            task = t * task_dev + a
            block, live = block_for(task, my_owner)
            factor = scale_ref[task].astype(jnp.float32) / denominator
            factor = jnp.where(live == 1, factor, 0.0)
            local = block - my_owner * own_blocks
            weights.append([jnp.where(local == j, factor, 0.0) for j in range(own_blocks)])
        pieces = [p.astype(jnp.float32) for p in pieces()]
        for j in range(own_blocks):
            total = raw[s, j]
            for a in range(task_dev):
                total = total + weights[a][j] * pieces[a]
            raw[s, j] = total

    add_in((0, 0), lambda: [held[a, chosen[0, a]] for a in range(task_dev)])
    for d, off in enumerate(owner_offsets):
        def pieces(d=d):
            sends[d].wait_recv()
            return [incoming[d, a] for a in range(task_dev)]
        add_in(off, pieces)

    merged_sum = jnp.zeros((rows, LANES), jnp.float32)
    for g in range(groups):
        for j in range(own_blocks):
            value = raw[g, j]
            merged_sum = merged_sum + fold(value * value)
    stat_mine[1] = merged_sum

    stats = []
    for e, off in enumerate(stat_offsets):
        copy = pltpu.make_async_remote_copy(
            src_ref=stat_mine, dst_ref=stat_in.at[e],
            send_sem=stat_send.at[e], recv_sem=stat_recv.at[e],
            device_id=stat_at(off), device_id_type=MESH,
        )
        copy.start()
        stats.append(copy)
    base_total, merged_total = base_sum, merged_sum
    for e in range(len(stat_offsets)):
        stats[e].wait_recv()
        base_total = base_total + stat_in[e, 0]
        merged_total = merged_total + stat_in[e, 1]
    base_total = jnp.sum(base_total, axis=(0, 1), keepdims=True)
    merged_total = jnp.sum(merged_total, axis=(0, 1), keepdims=True)
    ratio = jnp.sqrt((base_total + epsilon) / (merged_total + epsilon))

    pairs = n_rep // 2
    pair, core = my_rep // 2, lax.rem(my_rep, 2)
    sibling = (my_task, my_shard, pair * 2 + 1 - core)

    def columns(g, rep):
        col = pl.multiple_of(g * group_cols + rep * width, width)
        return out_ref.at[:, :, pl.ds(col, width)]

    far, near, passed, keeps = [], [], [], []
    for g in range(groups):
        for j in range(own_blocks):
            mine[g, j] = (raw[g, j] * ratio).astype(jnp.bfloat16)
        for k in range(1, pairs):
            copy = pltpu.make_async_remote_copy(
                src_ref=mine.at[g], dst_ref=columns(g, my_rep),
                send_sem=far_send.at[g, k - 1], recv_sem=far_recv.at[g, k - 1],
                device_id=(my_task, my_shard, lax.rem(pair + k, pairs) * 2 + core), device_id_type=MESH,
            )
            copy.start()
            far.append((g, k, copy))
        copy = pltpu.make_async_remote_copy(
            src_ref=mine.at[g], dst_ref=columns(g, my_rep),
            send_sem=near_send.at[g], recv_sem=near_recv.at[g],
            device_id=sibling, device_id_type=MESH,
        )
        copy.start()
        near.append(copy)
        copy = pltpu.make_async_copy(mine.at[g], columns(g, my_rep), keep_sems.at[g])
        copy.start()
        keeps.append(copy)
    for g, k, copy in far:
        copy.wait_recv()
        part = columns(g, lax.rem(pair - k + pairs, pairs) * 2 + core)
        copy = pltpu.make_async_remote_copy(
            src_ref=part, dst_ref=part,
            send_sem=pass_send.at[g, k - 1], recv_sem=pass_recv.at[g, k - 1],
            device_id=sibling, device_id_type=MESH,
        )
        copy.start()
        passed.append(copy)
    for copy in near + passed:
        copy.wait_recv()
    for copy in keeps:
        copy.wait()
    for copy in sends + stats + [c for _, _, c in far] + near + passed:
        copy.wait_send()


def solution(mesh):
    n_task, n_shard, n_rep = mesh.shape["task"], mesh.shape["shard"], mesh.shape["rep"]

    def shards(deltas, base, sel_index, sel_count, scale_num):
        task_dev, nb_all, rows, width = deltas.shape
        own_blocks, _, groups, _ = base.shape
        layer_tasks = nb_all // LAYERS // own_blocks // n_shard
        dims = (n_task, n_shard, n_rep, layer_tasks)
        peers, group = offset_peers(*dims)
        hbm = pl.BlockSpec(memory_space=pltpu.HBM)
        return pl.pallas_call(
            functools.partial(kernel, dims),
            out_shape=jax.ShapeDtypeStruct((own_blocks, rows, groups * n_rep * width), jnp.bfloat16),
            in_specs=[hbm] * 5,
            out_specs=pl.BlockSpec(memory_space=pl.ANY),
            scratch_shapes=[
                pltpu.SMEM(sel_index.shape, jnp.int32),
                pltpu.SMEM(sel_count.shape, jnp.int32),
                pltpu.SMEM(scale_num.shape, jnp.int32),
                pltpu.VMEM(deltas.shape, jnp.bfloat16),
                pltpu.VMEM(base.shape, jnp.bfloat16),
                pltpu.VMEM((len(peers), task_dev, rows, width), jnp.bfloat16),
                pltpu.VMEM((len(peers), task_dev, rows, width), jnp.bfloat16),
                pltpu.VMEM((groups, own_blocks, rows, width), jnp.float32),
                pltpu.VMEM((groups, own_blocks, rows, width), jnp.bfloat16),
                pltpu.VMEM((2, rows, LANES), jnp.float32),
                pltpu.VMEM((len(group), 2, rows, LANES), jnp.float32),
                pltpu.SemaphoreType.DMA((3,)),
                pltpu.SemaphoreType.DMA((task_dev,)),
                pltpu.SemaphoreType.DMA,
                pltpu.SemaphoreType.DMA((len(peers),)),
                pltpu.SemaphoreType.DMA((len(peers),)),
                pltpu.SemaphoreType.DMA((len(group),)),
                pltpu.SemaphoreType.DMA((len(group),)),
                pltpu.SemaphoreType.DMA((groups, n_rep // 2)),
                pltpu.SemaphoreType.DMA((groups, n_rep // 2)),
                pltpu.SemaphoreType.DMA((groups,)),
                pltpu.SemaphoreType.DMA((groups,)),
                pltpu.SemaphoreType.DMA((groups, n_rep // 2)),
                pltpu.SemaphoreType.DMA((groups, n_rep // 2)),
                pltpu.SemaphoreType.DMA((groups,)),
            ],
            compiler_params=pltpu.CompilerParams(collective_id=0, has_side_effects=True, vmem_limit_bytes=16 * 1024 * 1024),
        )(sel_index, sel_count, scale_num, deltas, base)

    placed = (
        P("task", None, None, ("shard", "rep")),
        P(("task", "shard"), None, None, "rep"),
        P(),
        P(),
        P(),
    )
    return jax.shard_map(
        shards,
        mesh=mesh,
        in_specs=placed,
        out_specs=P(("task", "shard"), None, None),
        check_vma=False,
    )
```

```python
import functools

import jax
import jax.numpy as jnp
from jax import lax
from jax.experimental import pallas as pl
from jax.experimental.pallas import tpu as pltpu
from jax.sharding import PartitionSpec as P

LAYERS = 4
LANES = 128
MESH = pl.DeviceIdType.MESH

denominator = 8.0
epsilon = 1e-06


def offset_peers(n_task, n_shard, n_rep, layer_tasks):
    order = sorted(range(n_task), key=lambda a: (-min(a, n_task - a), -a))
    owners = [(a, b) for a in order for b in range(n_shard) if a or b]
    group = [(a, b, c) for a in range(layer_tasks) for b in range(n_shard) for c in range(n_rep)][1:]
    return owners, group


def kernel(
    dims, index_hbm, count_hbm, scale_hbm, deltas_ref, base_ref, out_ref,
    index_ref, count_ref, scale_ref,
    held, base_held, outgoing, incoming, raw, mine, stat_mine, stat_in,
    table_sems, load_sems, base_sem, send_sems, recv_sems, stat_send, stat_recv,
    far_send, far_recv, near_send, near_recv, pass_send, pass_recv, keep_sems,
):
    n_task, n_shard, n_rep, layer_tasks = dims
    task_dev, nb_all, rows, width = deltas_ref.shape
    groups, own_blocks = raw.shape[:2]
    group_cols = out_ref.shape[2] // groups
    kmax = index_ref.shape[1]
    owner_offsets, stat_offsets = offset_peers(n_task, n_shard, n_rep, layer_tasks)

    my_task = lax.axis_index("task")
    my_shard = lax.axis_index("shard")
    my_rep = lax.axis_index("rep")

    tables = []
    for i, (src, dst) in enumerate(
        ((index_hbm, index_ref), (count_hbm, count_ref), (scale_hbm, scale_ref))
    ):
        copy = pltpu.make_async_copy(src, dst, table_sems.at[i])
        copy.start()
        tables.append(copy)
    loads = []
    for a in range(task_dev):
        copy = pltpu.make_async_copy(deltas_ref.at[a], held.at[a], load_sems.at[a])
        copy.start()
        loads.append(copy)
    base_copy = pltpu.make_async_copy(base_ref, base_held, base_sem)
    base_copy.start()

    def owner_at(off, sign=1):
        t = lax.rem(my_task + sign * off[0] + n_task, n_task)
        s = lax.rem(my_shard + sign * off[1] + n_shard, n_shard)
        return t, s

    layer_first = (my_task // layer_tasks) * layer_tasks

    def stat_at(off):
        t = layer_first + lax.rem(my_task - layer_first + off[0], layer_tasks)
        s = lax.rem(my_shard + off[1], n_shard)
        r = lax.rem(my_rep + off[2], n_rep)
        return t, s, r

    barrier = pltpu.get_barrier_semaphore()
    for off in owner_offsets:
        t, s = owner_at(off)
        pl.semaphore_signal(barrier, inc=1, device_id=(t, s, my_rep), device_id_type=MESH)
    extra = [o for o in stat_offsets if o[2] != 0]
    for off in extra:
        pl.semaphore_signal(barrier, inc=1, device_id=stat_at(off), device_id_type=MESH)

    for copy in tables:
        copy.wait()

    def block_for(task, owner):
        count = count_ref[task]

        def step(k, carry):
            block, live = carry
            entry = index_ref[task, k]
            hit = (k < count) & (entry // own_blocks == owner)
            return jnp.where(hit, entry, block), jnp.where(hit, 1, live)

        start = (owner * own_blocks, jnp.int32(0))
        return lax.fori_loop(0, kmax, step, start, unroll=kmax <= 8)

    chosen = {}
    for d, off in enumerate([(0, 0)] + owner_offsets):
        t, s = owner_at(off)
        for a in range(task_dev):
            chosen[d, a] = block_for(my_task * task_dev + a, t * n_shard + s)[0]

    for copy in loads:
        copy.wait()

    for d, off in enumerate(owner_offsets):
        for a in range(task_dev):
            outgoing[d, a] = held[a, chosen[d + 1, a]]

    pl.semaphore_wait(barrier, len(owner_offsets) + len(extra))

    sends = []
    for d, off in enumerate(owner_offsets):
        t, s = owner_at(off)
        copy = pltpu.make_async_remote_copy(
            src_ref=outgoing.at[d], dst_ref=incoming.at[d],
            send_sem=send_sems.at[d], recv_sem=recv_sems.at[d],
            device_id=(t, s, my_rep), device_id_type=MESH,
        )
        copy.start()
        sends.append(copy)

    def fold(values):
        total = values[:, 0:LANES]
        for c in range(LANES, values.shape[1], LANES):
            total = total + values[:, c:c + LANES]
        return total

    base_copy.wait()
    base_sum = jnp.zeros((rows, LANES), jnp.float32)
    for g in range(groups):
        for j in range(own_blocks):
            wide = base_held[j, :, g, :].astype(jnp.float32)
            raw[g, j] = wide
            base_sum = base_sum + fold(wide * wide)
    stat_mine[0] = base_sum

    my_owner = my_task * n_shard + my_shard

    def add_in(off, pieces):
        t, s = owner_at(off, -1)
        weights = []
        for a in range(task_dev):
            task = t * task_dev + a
            block, live = block_for(task, my_owner)
            factor = scale_ref[task].astype(jnp.float32) / denominator
            factor = jnp.where(live == 1, factor, 0.0)
            local = block - my_owner * own_blocks
            weights.append([jnp.where(local == j, factor, 0.0) for j in range(own_blocks)])
        pieces = [p.astype(jnp.float32) for p in pieces()]
        for j in range(own_blocks):
            total = raw[s, j]
            for a in range(task_dev):
                total = total + weights[a][j] * pieces[a]
            raw[s, j] = total

    add_in((0, 0), lambda: [held[a, chosen[0, a]] for a in range(task_dev)])
    for d, off in enumerate(owner_offsets):
        def pieces(d=d):
            sends[d].wait_recv()
            return [incoming[d, a] for a in range(task_dev)]
        add_in(off, pieces)

    merged_sum = jnp.zeros((rows, LANES), jnp.float32)
    for g in range(groups):
        for j in range(own_blocks):
            value = raw[g, j]
            merged_sum = merged_sum + fold(value * value)
    stat_mine[1] = merged_sum

    stats = []
    for e, off in enumerate(stat_offsets):
        copy = pltpu.make_async_remote_copy(
            src_ref=stat_mine, dst_ref=stat_in.at[e],
            send_sem=stat_send.at[e], recv_sem=stat_recv.at[e],
            device_id=stat_at(off), device_id_type=MESH,
        )
        copy.start()
        stats.append(copy)
    base_total, merged_total = base_sum, merged_sum
    for e in range(len(stat_offsets)):
        stats[e].wait_recv()
        base_total = base_total + stat_in[e, 0]
        merged_total = merged_total + stat_in[e, 1]
    base_total = jnp.sum(base_total, axis=(0, 1), keepdims=True)
    merged_total = jnp.sum(merged_total, axis=(0, 1), keepdims=True)
    ratio = jnp.sqrt((base_total + epsilon) / (merged_total + epsilon))

    pairs = n_rep // 2
    pair, core = my_rep // 2, lax.rem(my_rep, 2)
    sibling = (my_task, my_shard, pair * 2 + 1 - core)

    def columns(g, rep):
        col = pl.multiple_of(g * group_cols + rep * width, width)
        return out_ref.at[:, :, pl.ds(col, width)]

    far, near, passed, keeps = [], [], [], []
    for g in range(groups):
        for j in range(own_blocks):
            mine[g, j] = (raw[g, j] * ratio).astype(jnp.bfloat16)
        for k in range(1, pairs):
            copy = pltpu.make_async_remote_copy(
                src_ref=mine.at[g], dst_ref=columns(g, my_rep),
                send_sem=far_send.at[g, k - 1], recv_sem=far_recv.at[g, k - 1],
                device_id=(my_task, my_shard, lax.rem(pair + k, pairs) * 2 + core), device_id_type=MESH,
            )
            copy.start()
            far.append((g, k, copy))
        copy = pltpu.make_async_remote_copy(
            src_ref=mine.at[g], dst_ref=columns(g, my_rep),
            send_sem=near_send.at[g], recv_sem=near_recv.at[g],
            device_id=sibling, device_id_type=MESH,
        )
        copy.start()
        near.append(copy)
        copy = pltpu.make_async_copy(mine.at[g], columns(g, my_rep), keep_sems.at[g])
        copy.start()
        keeps.append(copy)
    for g, k, copy in far:
        copy.wait_recv()
        part = columns(g, lax.rem(pair - k + pairs, pairs) * 2 + core)
        copy = pltpu.make_async_remote_copy(
            src_ref=part, dst_ref=part,
            send_sem=pass_send.at[g, k - 1], recv_sem=pass_recv.at[g, k - 1],
            device_id=sibling, device_id_type=MESH,
        )
        copy.start()
        passed.append(copy)
    for copy in near + passed:
        copy.wait_recv()
    for copy in keeps:
        copy.wait()
    for copy in sends + stats + [c for _, _, c in far] + near + passed:
        copy.wait_send()


def solution(mesh):
    n_task, n_shard, n_rep = mesh.shape["task"], mesh.shape["shard"], mesh.shape["rep"]

    def shards(deltas, base, sel_index, sel_count, scale_num):
        task_dev, nb_all, rows, width = deltas.shape
        own_blocks, _, groups, _ = base.shape
        layer_tasks = nb_all // LAYERS // own_blocks // n_shard
        dims = (n_task, n_shard, n_rep, layer_tasks)
        peers, group = offset_peers(*dims)
        hbm = pl.BlockSpec(memory_space=pltpu.HBM)
        return pl.pallas_call(
            functools.partial(kernel, dims),
            out_shape=jax.ShapeDtypeStruct((own_blocks, rows, groups * n_rep * width), jnp.bfloat16),
            in_specs=[hbm] * 5,
            out_specs=pl.BlockSpec(memory_space=pl.ANY),
            scratch_shapes=[
                pltpu.SMEM(sel_index.shape, jnp.int32),
                pltpu.SMEM(sel_count.shape, jnp.int32),
                pltpu.SMEM(scale_num.shape, jnp.int32),
                pltpu.VMEM(deltas.shape, jnp.bfloat16),
                pltpu.VMEM(base.shape, jnp.bfloat16),
                pltpu.VMEM((len(peers), task_dev, rows, width), jnp.bfloat16),
                pltpu.VMEM((len(peers), task_dev, rows, width), jnp.bfloat16),
                pltpu.VMEM((groups, own_blocks, rows, width), jnp.float32),
                pltpu.VMEM((groups, own_blocks, rows, width), jnp.bfloat16),
                pltpu.VMEM((2, rows, LANES), jnp.float32),
                pltpu.VMEM((len(group), 2, rows, LANES), jnp.float32),
                pltpu.SemaphoreType.DMA((3,)),
                pltpu.SemaphoreType.DMA((task_dev,)),
                pltpu.SemaphoreType.DMA,
                pltpu.SemaphoreType.DMA((len(peers),)),
                pltpu.SemaphoreType.DMA((len(peers),)),
                pltpu.SemaphoreType.DMA((len(group),)),
                pltpu.SemaphoreType.DMA((len(group),)),
                pltpu.SemaphoreType.DMA((groups, n_rep // 2)),
                pltpu.SemaphoreType.DMA((groups, n_rep // 2)),
                pltpu.SemaphoreType.DMA((groups,)),
                pltpu.SemaphoreType.DMA((groups,)),
                pltpu.SemaphoreType.DMA((groups, n_rep // 2)),
                pltpu.SemaphoreType.DMA((groups, n_rep // 2)),
                pltpu.SemaphoreType.DMA((groups,)),
            ],
            compiler_params=pltpu.CompilerParams(collective_id=0, has_side_effects=True, vmem_limit_bytes=16 * 1024 * 1024),
        )(*[pltpu.with_memory_space_constraint(x, pltpu.HBM) for x in (sel_index, sel_count, scale_num, deltas, base)])

    placed = (
        P("task", None, None, ("shard", "rep")),
        P(("task", "shard"), None, None, "rep"),
        P(),
        P(),
        P(),
    )
    return jax.shard_map(
        shards,
        mesh=mesh,
        in_specs=placed,
        out_specs=P(("task", "shard"), None, None),
        check_vma=False,
    )
```

```python
import functools

import jax
import jax.numpy as jnp
from jax import lax
from jax.experimental import pallas as pl
from jax.experimental.pallas import tpu as pltpu
from jax.sharding import PartitionSpec as P

LAYERS = 4
LANES = 128
EARLY = 5
MESH = pl.DeviceIdType.MESH

denominator = 8.0
epsilon = 1e-06


def offset_peers(n_task, n_shard, n_rep, layer_tasks):
    order = sorted(range(n_task), key=lambda a: (-min(a, n_task - a), -a))
    owners = [(a, b) for a in order for b in range(n_shard) if a or b]
    group = [(a, b, c) for a in range(layer_tasks) for b in range(n_shard) for c in range(n_rep)][1:]
    return owners, group


def kernel(
    dims, index_hbm, count_hbm, scale_hbm, deltas_ref, base_ref, out_ref,
    index_ref, count_ref, scale_ref,
    held, base_held, outgoing, incoming, raw, mine, stat_mine, stat_in,
    own, twin_base, twin_in, twin_raw, twin_mine, twin_send, twin_recv, side_send, side_recv, side_keep,
    table_sems, load_sems, base_sem, send_sems, recv_sems, stat_send, stat_recv,
    far_send, far_recv, near_send, near_recv, pass_send, pass_recv, keep_sems,
):
    n_task, n_shard, n_rep, layer_tasks = dims
    task_dev, nb_all, rows, width = deltas_ref.shape
    groups, own_blocks = raw.shape[:2]
    group_cols = out_ref.shape[2] // groups
    kmax = index_ref.shape[1]
    owner_offsets, stat_offsets = offset_peers(n_task, n_shard, n_rep, layer_tasks)

    my_task = lax.axis_index("task")
    my_shard = lax.axis_index("shard")
    my_rep = lax.axis_index("rep")

    def owner_at(off, sign=1):
        t = lax.rem(my_task + sign * off[0] + n_task, n_task)
        s = lax.rem(my_shard + sign * off[1] + n_shard, n_shard)
        return t, s

    layer_first = (my_task // layer_tasks) * layer_tasks

    def stat_at(off):
        t = layer_first + lax.rem(my_task - layer_first + off[0], layer_tasks)
        s = lax.rem(my_shard + off[1], n_shard)
        r = lax.rem(my_rep + off[2], n_rep)
        return t, s, r

    barrier = pltpu.get_barrier_semaphore()
    for off in owner_offsets:
        t, s = owner_at(off)
        pl.semaphore_signal(barrier, inc=1, device_id=(t, s, my_rep), device_id_type=MESH)
    extra = [o for o in stat_offsets if o[2] != 0]
    for off in extra:
        pl.semaphore_signal(barrier, inc=1, device_id=stat_at(off), device_id_type=MESH)

    tables = []
    for i, (src, dst) in enumerate(
        ((index_hbm, index_ref), (count_hbm, count_ref), (scale_hbm, scale_ref))
    ):
        copy = pltpu.make_async_copy(src, dst, table_sems.at[i])
        copy.start()
        tables.append(copy)
    loads = []
    for a in range(task_dev):
        copy = pltpu.make_async_copy(deltas_ref.at[a], held.at[a], load_sems.at[a])
        copy.start()
        loads.append(copy)
    base_copy = pltpu.make_async_copy(base_ref, base_held, base_sem)
    base_copy.start()

    for copy in tables:
        copy.wait()

    def block_for(task, wanted):
        count = count_ref[task]

        def step(k, carry):
            entry = index_ref[task, k]
            owner = jnp.where(k < count, lax.div(entry, own_blocks), -1)
            return tuple(
                (jnp.where(owner == o, entry, block), jnp.where(owner == o, 1, live))
                for o, (block, live) in zip(wanted, carry)
            )

        start = tuple((o * own_blocks, jnp.int32(0)) for o in wanted)
        if kmax > 8:
            return lax.fori_loop(0, kmax, step, start)
        for k in range(kmax):
            start = step(k, start)
        return start

    slots = [(0, 0)] + owner_offsets
    wanted = []
    for off in slots:
        t, s = owner_at(off)
        wanted.append(t * n_shard + s)
    chosen = {}
    for a in range(task_dev):
        for d, (block, _) in enumerate(block_for(my_task * task_dev + a, wanted)):
            chosen[d, a] = block

    for copy in loads:
        copy.wait()

    for d, off in enumerate(owner_offsets):
        for a in range(task_dev):
            outgoing[d, a] = held[a, chosen[d + 1, a]]
    for a in range(task_dev):
        own[a] = held[a, chosen[0, a]][:, :own.shape[2]]

    pl.semaphore_wait(barrier, len(owner_offsets) + len(extra))

    sends = []
    for d, off in enumerate(owner_offsets):
        t, s = owner_at(off)
        copy = pltpu.make_async_remote_copy(
            src_ref=outgoing.at[d], dst_ref=incoming.at[d],
            send_sem=send_sems.at[d], recv_sem=recv_sems.at[d],
            device_id=(t, s, my_rep), device_id_type=MESH,
        )
        copy.start()
        sends.append(copy)

    pairs = n_rep // 2
    pair, core = my_rep // 2, lax.rem(my_rep, 2)
    twin_rep = lax.rem(pair + 1, pairs) * 2 + core
    early = twin_raw.shape[3]

    def to_twin(i, src, dst):
        copy = pltpu.make_async_remote_copy(
            src_ref=src, dst_ref=dst, send_sem=twin_send.at[i], recv_sem=twin_recv.at[i],
            device_id=(my_task, my_shard, twin_rep), device_id_type=MESH,
        )
        copy.start()
        return copy

    twin_base_copy = to_twin(len(slots), base_ref.at[:, :, :, pl.ds(0, early)], twin_base)
    twins = [to_twin(0, own, twin_in.at[0])]

    def fold(values):
        total = values[:, 0:LANES]
        for c in range(LANES, values.shape[1], LANES):
            total = total + values[:, c:c + LANES]
        return total

    base_copy.wait()
    base_sum = jnp.zeros((rows, LANES), jnp.float32)
    for g in range(groups):
        for j in range(own_blocks):
            wide = base_held[j, :, g, :].astype(jnp.float32)
            raw[g, j] = wide
            base_sum = base_sum + fold(wide * wide)
    stat_mine[0:1] = jnp.sum(base_sum, axis=0, keepdims=True)

    my_owner = my_task * n_shard + my_shard

    weights, sources = [], []
    for off in slots:
        t, s = owner_at(off, -1)
        sources.append(s)
        weights.append([])
        for a in range(task_dev):
            task = t * task_dev + a
            block, live = block_for(task, [my_owner])[0]
            factor = scale_ref[task].astype(jnp.float32) / denominator
            factor = jnp.where(live == 1, factor, 0.0)
            local = block - my_owner * own_blocks
            weights[-1].append([jnp.where(local == j, factor, 0.0) for j in range(own_blocks)])

    def add_in(total_ref, d, pieces):
        pieces = [p.astype(jnp.float32) for p in pieces]
        for j in range(own_blocks):
            total = total_ref[sources[d], j]
            for a in range(task_dev):
                total = total + weights[d][a][j] * pieces[a]
            total_ref[sources[d], j] = total

    def widen_twin():
        twin_base_copy.wait_recv()
        for g in range(groups):
            for j in range(own_blocks):
                twin_raw[g, j] = twin_base[j, :, g, :].astype(jnp.float32)

    def add_twin(i, d):
        twins[i].wait_recv()
        add_in(twin_raw, d, [twin_in[d, a] for a in range(task_dev)])

    add_in(raw, 0, [held[a, chosen[0, a]] for a in range(task_dev)])
    last = len(slots) - 1
    arrivals = [last] + list(range(1, last))
    order = [0] + arrivals
    lag = 3
    for i, d in enumerate(arrivals):
        sends[d - 1].wait_recv()
        twins.append(to_twin(d, incoming.at[d - 1, :, :, pl.ds(0, early)], twin_in.at[d]))
        add_in(raw, d, [incoming[d - 1, a] for a in range(task_dev)])
        if i == lag - 1:
            widen_twin()
        if i >= lag:
            add_twin(i - lag, order[i - lag])

    merged_sum = jnp.zeros((rows, LANES), jnp.float32)
    for g in range(groups):
        for j in range(own_blocks):
            value = raw[g, j]
            merged_sum = merged_sum + fold(value * value)
    stat_mine[1:2] = jnp.sum(merged_sum, axis=0, keepdims=True)

    stats = []
    for e, off in enumerate(stat_offsets):
        copy = pltpu.make_async_remote_copy(
            src_ref=stat_mine, dst_ref=stat_in.at[e],
            send_sem=stat_send.at[e], recv_sem=stat_recv.at[e],
            device_id=stat_at(off), device_id_type=MESH,
        )
        copy.start()
        stats.append(copy)
    for i in range(len(arrivals) - lag, len(order)):
        add_twin(i, order[i])
    totals = stat_mine[...]
    for e in range(len(stat_offsets)):
        stats[e].wait_recv()
        totals = totals + stat_in[e]
    totals = jnp.sum(totals, axis=1, keepdims=True)
    base_total, merged_total = totals[0:1], totals[1:2]
    ratio = jnp.sqrt((base_total + epsilon) / (merged_total + epsilon))

    def columns(g, rep, first, size):
        col = pl.multiple_of(g * group_cols + rep * width + first, LANES)
        return out_ref.at[:, :, pl.ds(col, size)]

    def scaled(ref, g, j, first, size):
        return (ref[g, j, :, pl.ds(first, size)] * ratio).astype(jnp.bfloat16)

    def to_core(src, dst, send, recv, rep):
        copy = pltpu.make_async_remote_copy(
            src_ref=src, dst_ref=dst, send_sem=send, recv_sem=recv,
            device_id=(my_task, my_shard, rep), device_id_type=MESH,
        )
        copy.start()
        return copy

    sibling_rep = pair * 2 + 1 - core
    late = width - early
    far, near, keeps = [], [], []
    for g in range(groups):
        for j in range(own_blocks):
            mine[g, j, :, pl.ds(early, late)] = scaled(raw, g, j, early, late)
        far.append(to_core(
            mine.at[g, :, :, pl.ds(early, late)], columns(g, my_rep, early, late),
            far_send.at[g], far_recv.at[g], twin_rep,
        ))
    for g in range(groups):
        for j in range(own_blocks):
            mine[g, j, :, pl.ds(0, early)] = scaled(raw, g, j, 0, early)
            twin_mine[g, j] = scaled(twin_raw, g, j, 0, early)
        part = columns(g, my_rep, 0, width)
        near.append(to_core(mine.at[g], part, near_send.at[g], near_recv.at[g], sibling_rep))
        keeps.append(pltpu.make_async_copy(mine.at[g], part, keep_sems.at[g]))
        keeps[-1].start()
        part = columns(g, twin_rep, 0, early)
        near.append(to_core(twin_mine.at[g], part, side_send.at[g], side_recv.at[g], sibling_rep))
        keeps.append(pltpu.make_async_copy(twin_mine.at[g], part, side_keep.at[g]))
        keeps[-1].start()
    passed = []
    for g in range(groups):
        far[g].wait_recv()
        part = columns(g, twin_rep, early, late)
        passed.append(to_core(part, part, pass_send.at[g], pass_recv.at[g], sibling_rep))
    for copy in near + passed:
        copy.wait_recv()
    for copy in keeps:
        copy.wait()
    for copy in sends + twins + [twin_base_copy] + stats + far + near + passed:
        copy.wait_send()


def solution(mesh):
    n_task, n_shard, n_rep = mesh.shape["task"], mesh.shape["shard"], mesh.shape["rep"]

    def shards(deltas, base, sel_index, sel_count, scale_num):
        task_dev, nb_all, rows, width = deltas.shape
        own_blocks, _, groups, _ = base.shape
        layer_tasks = nb_all // LAYERS // own_blocks // n_shard
        dims = (n_task, n_shard, n_rep, layer_tasks)
        peers, group = offset_peers(*dims)
        early = width * EARLY // 8 // LANES * LANES
        hbm = pl.BlockSpec(memory_space=pltpu.HBM)
        return pl.pallas_call(
            functools.partial(kernel, dims),
            out_shape=jax.ShapeDtypeStruct((own_blocks, rows, groups * n_rep * width), jnp.bfloat16),
            in_specs=[hbm] * 5,
            out_specs=pl.BlockSpec(memory_space=pl.ANY),
            scratch_shapes=[
                pltpu.SMEM(sel_index.shape, jnp.int32),
                pltpu.SMEM(sel_count.shape, jnp.int32),
                pltpu.SMEM(scale_num.shape, jnp.int32),
                pltpu.VMEM(deltas.shape, jnp.bfloat16),
                pltpu.VMEM(base.shape, jnp.bfloat16),
                pltpu.VMEM((len(peers), task_dev, rows, width), jnp.bfloat16),
                pltpu.VMEM((len(peers), task_dev, rows, width), jnp.bfloat16),
                pltpu.VMEM((groups, own_blocks, rows, width), jnp.float32),
                pltpu.VMEM((groups, own_blocks, rows, width), jnp.bfloat16),
                pltpu.VMEM((2, LANES), jnp.float32),
                pltpu.VMEM((len(group), 2, LANES), jnp.float32),
                pltpu.VMEM((task_dev, rows, early), jnp.bfloat16),
                pltpu.VMEM((own_blocks, rows, groups, early), jnp.bfloat16),
                pltpu.VMEM((len(peers) + 1, task_dev, rows, early), jnp.bfloat16),
                pltpu.VMEM((groups, own_blocks, rows, early), jnp.float32),
                pltpu.VMEM((groups, own_blocks, rows, early), jnp.bfloat16),
                pltpu.SemaphoreType.DMA((len(peers) + 2,)),
                pltpu.SemaphoreType.DMA((len(peers) + 2,)),
                pltpu.SemaphoreType.DMA((groups,)),
                pltpu.SemaphoreType.DMA((groups,)),
                pltpu.SemaphoreType.DMA((groups,)),
                pltpu.SemaphoreType.DMA((3,)),
                pltpu.SemaphoreType.DMA((task_dev,)),
                pltpu.SemaphoreType.DMA,
                pltpu.SemaphoreType.DMA((len(peers),)),
                pltpu.SemaphoreType.DMA((len(peers),)),
                pltpu.SemaphoreType.DMA((len(group),)),
                pltpu.SemaphoreType.DMA((len(group),)),
                pltpu.SemaphoreType.DMA((groups,)),
                pltpu.SemaphoreType.DMA((groups,)),
                pltpu.SemaphoreType.DMA((groups,)),
                pltpu.SemaphoreType.DMA((groups,)),
                pltpu.SemaphoreType.DMA((groups,)),
                pltpu.SemaphoreType.DMA((groups,)),
                pltpu.SemaphoreType.DMA((groups,)),
            ],
            compiler_params=pltpu.CompilerParams(collective_id=0, has_side_effects=True, vmem_limit_bytes=16 * 1024 * 1024),
        )(*[pltpu.with_memory_space_constraint(x, pltpu.HBM) for x in (sel_index, sel_count, scale_num, deltas, base)])

    placed = (
        P("task", None, None, ("shard", "rep")),
        P(("task", "shard"), None, None, "rep"),
        P(),
        P(),
        P(),
    )
    return jax.shard_map(
        shards,
        mesh=mesh,
        in_specs=placed,
        out_specs=P(("task", "shard"), None, None),
        check_vma=False,
    )
```

```python
import functools

import jax
import jax.numpy as jnp
from jax import lax
from jax.experimental import pallas as pl
from jax.experimental.pallas import tpu as pltpu
from jax.sharding import PartitionSpec as P

LAYERS = 4
LANES = 128
EARLY = 6
MESH = pl.DeviceIdType.MESH

denominator = 8.0
epsilon = 1e-06


def offset_peers(n_task, n_shard, n_rep, layer_tasks):
    order = sorted(range(n_task), key=lambda a: (-min(a, n_task - a), -a))
    owners = [(a, b) for a in order for b in reversed(range(n_shard)) if a or b]
    group = [(a, b, c) for a in range(layer_tasks) for b in range(n_shard) for c in range(n_rep)][1:]
    return owners, group


def kernel(
    dims, index_hbm, count_hbm, scale_hbm, deltas_ref, base_ref, out_ref,
    index_ref, count_ref, scale_ref,
    held, base_held, outgoing, incoming, raw, mine, stat_mine, stat_in,
    own, twin_base, twin_in, twin_raw, twin_mine, twin_send, twin_recv, side_send, side_recv, side_keep,
    table_sems, load_sems, base_sem, send_sems, recv_sems, stat_send, stat_recv,
    far_send, far_recv, near_send, near_recv, pass_send, pass_recv, keep_sems,
):
    n_task, n_shard, n_rep, layer_tasks = dims
    task_dev, nb_all, rows, width = deltas_ref.shape
    groups, own_blocks = raw.shape[:2]
    group_cols = out_ref.shape[2] // groups
    kmax = index_ref.shape[1]
    owner_offsets, stat_offsets = offset_peers(n_task, n_shard, n_rep, layer_tasks)

    my_task = lax.axis_index("task")
    my_shard = lax.axis_index("shard")
    my_rep = lax.axis_index("rep")

    def owner_at(off, sign=1):
        t = lax.rem(my_task + sign * off[0] + n_task, n_task)
        s = lax.rem(my_shard + sign * off[1] + n_shard, n_shard)
        return t, s

    layer_first = (my_task // layer_tasks) * layer_tasks

    def stat_at(off):
        t = layer_first + lax.rem(my_task - layer_first + off[0], layer_tasks)
        s = lax.rem(my_shard + off[1], n_shard)
        r = lax.rem(my_rep + off[2], n_rep)
        return t, s, r

    barrier = pltpu.get_barrier_semaphore()
    for off in owner_offsets:
        t, s = owner_at(off)
        pl.semaphore_signal(barrier, inc=1, device_id=(t, s, my_rep), device_id_type=MESH)
    extra = [o for o in stat_offsets if o[2] != 0]
    for off in extra:
        pl.semaphore_signal(barrier, inc=1, device_id=stat_at(off), device_id_type=MESH)

    tables = []
    for i, (src, dst) in enumerate(
        ((index_hbm, index_ref), (count_hbm, count_ref), (scale_hbm, scale_ref))
    ):
        copy = pltpu.make_async_copy(src, dst, table_sems.at[i])
        copy.start()
        tables.append(copy)
    loads = []
    for a in range(task_dev):
        copy = pltpu.make_async_copy(deltas_ref.at[a], held.at[a], load_sems.at[a])
        copy.start()
        loads.append(copy)
    base_copy = pltpu.make_async_copy(base_ref, base_held, base_sem)
    base_copy.start()

    for copy in tables:
        copy.wait()

    def block_for(task, wanted):
        count = count_ref[task]

        def step(k, carry):
            entry = index_ref[task, k]
            owner = jnp.where(k < count, lax.div(entry, own_blocks), -1)
            return tuple(
                (jnp.where(owner == o, entry, block), jnp.where(owner == o, 1, live))
                for o, (block, live) in zip(wanted, carry)
            )

        start = tuple((o * own_blocks, jnp.int32(0)) for o in wanted)
        if kmax > 8:
            return lax.fori_loop(0, kmax, step, start)
        for k in range(kmax):
            start = step(k, start)
        return start

    slots = [(0, 0)] + owner_offsets
    wanted = []
    for off in slots:
        t, s = owner_at(off)
        wanted.append(t * n_shard + s)
    chosen = {}
    for a in range(task_dev):
        for d, (block, _) in enumerate(block_for(my_task * task_dev + a, wanted)):
            chosen[d, a] = block

    for copy in loads:
        copy.wait()

    for d, off in enumerate(owner_offsets):
        for a in range(task_dev):
            outgoing[d, a] = held[a, chosen[d + 1, a]]
    for a in range(task_dev):
        own[a] = held[a, chosen[0, a]][:, :own.shape[2]]

    pl.semaphore_wait(barrier, len(owner_offsets) + len(extra))

    sends = []
    for d, off in enumerate(owner_offsets):
        t, s = owner_at(off)
        copy = pltpu.make_async_remote_copy(
            src_ref=outgoing.at[d], dst_ref=incoming.at[d],
            send_sem=send_sems.at[d], recv_sem=recv_sems.at[d],
            device_id=(t, s, my_rep), device_id_type=MESH,
        )
        copy.start()
        sends.append(copy)

    pairs = n_rep // 2
    pair, core = my_rep // 2, lax.rem(my_rep, 2)
    twin_rep = lax.rem(pair + 1, pairs) * 2 + core
    early = twin_raw.shape[3]

    def to_twin(i, src, dst):
        copy = pltpu.make_async_remote_copy(
            src_ref=src, dst_ref=dst, send_sem=twin_send.at[i], recv_sem=twin_recv.at[i],
            device_id=(my_task, my_shard, twin_rep), device_id_type=MESH,
        )
        copy.start()
        return copy

    twin_base_copy = to_twin(len(slots), base_ref.at[:, :, :, pl.ds(0, early)], twin_base)
    twins = [to_twin(0, own, twin_in.at[0])]

    def fold(values):
        total = values[:, 0:LANES]
        for c in range(LANES, values.shape[1], LANES):
            total = total + values[:, c:c + LANES]
        return total

    base_copy.wait()
    base_sum = jnp.zeros((rows, LANES), jnp.float32)
    for g in range(groups):
        for j in range(own_blocks):
            wide = base_held[j, :, g, :].astype(jnp.float32)
            raw[g, j] = wide
            base_sum = base_sum + fold(wide * wide)
    stat_mine[0:1] = jnp.sum(base_sum, axis=0, keepdims=True)

    my_owner = my_task * n_shard + my_shard

    weights, sources = [], []
    for off in slots:
        t, s = owner_at(off, -1)
        sources.append(s)
        weights.append([])
        for a in range(task_dev):
            task = t * task_dev + a
            block, live = block_for(task, [my_owner])[0]
            factor = scale_ref[task].astype(jnp.float32) / denominator
            factor = jnp.where(live == 1, factor, 0.0)
            local = block - my_owner * own_blocks
            weights[-1].append([jnp.where(local == j, factor, 0.0) for j in range(own_blocks)])

    def add_in(total_ref, d, pieces):
        pieces = [p.astype(jnp.float32) for p in pieces]
        for j in range(own_blocks):
            total = total_ref[sources[d], j]
            for a in range(task_dev):
                total = total + weights[d][a][j] * pieces[a]
            total_ref[sources[d], j] = total

    def widen_twin():
        twin_base_copy.wait_recv()
        for g in range(groups):
            for j in range(own_blocks):
                twin_raw[g, j] = twin_base[j, :, g, :].astype(jnp.float32)

    def add_twin(i, d):
        twins[i].wait_recv()
        add_in(twin_raw, d, [twin_in[d, a] for a in range(task_dev)])

    add_in(raw, 0, [held[a, chosen[0, a]] for a in range(task_dev)])
    last = len(slots) - 1
    arrivals = [last] + list(range(1, last))
    order = [0] + arrivals
    lag = 3
    for i, d in enumerate(arrivals):
        sends[d - 1].wait_recv()
        twins.append(to_twin(d, incoming.at[d - 1, :, :, pl.ds(0, early)], twin_in.at[d]))
        add_in(raw, d, [incoming[d - 1, a] for a in range(task_dev)])
        if i == lag - 1:
            widen_twin()
        if i >= lag:
            add_twin(i - lag, order[i - lag])

    merged_sum = jnp.zeros((rows, LANES), jnp.float32)
    for g in range(groups):
        for j in range(own_blocks):
            value = raw[g, j]
            merged_sum = merged_sum + fold(value * value)
    stat_mine[1:2] = jnp.sum(merged_sum, axis=0, keepdims=True)

    stats = []
    for e, off in enumerate(stat_offsets):
        copy = pltpu.make_async_remote_copy(
            src_ref=stat_mine, dst_ref=stat_in.at[e],
            send_sem=stat_send.at[e], recv_sem=stat_recv.at[e],
            device_id=stat_at(off), device_id_type=MESH,
        )
        copy.start()
        stats.append(copy)
    for i in range(len(arrivals) - lag, len(order)):
        add_twin(i, order[i])
    totals = stat_mine[...]
    for e in range(len(stat_offsets)):
        stats[e].wait_recv()
        totals = totals + stat_in[e]
    totals = jnp.sum(totals, axis=1, keepdims=True)
    base_total, merged_total = totals[0:1], totals[1:2]
    ratio = jnp.sqrt((base_total + epsilon) / (merged_total + epsilon))

    def columns(g, rep, first, size):
        col = pl.multiple_of(g * group_cols + rep * width + first, LANES)
        return out_ref.at[:, :, pl.ds(col, size)]

    def scaled(ref, g, j, first, size):
        return (ref[g, j, :, pl.ds(first, size)] * ratio).astype(jnp.bfloat16)

    def to_core(src, dst, send, recv, rep):
        copy = pltpu.make_async_remote_copy(
            src_ref=src, dst_ref=dst, send_sem=send, recv_sem=recv,
            device_id=(my_task, my_shard, rep), device_id_type=MESH,
        )
        copy.start()
        return copy

    sibling_rep = pair * 2 + 1 - core
    late = width - early
    far, near, keeps = [], [], []
    for g in range(groups):
        for j in range(own_blocks):
            mine[g, j, :, pl.ds(early, late)] = scaled(raw, g, j, early, late)
        far.append(to_core(
            mine.at[g, :, :, pl.ds(early, late)], columns(g, my_rep, early, late),
            far_send.at[g], far_recv.at[g], twin_rep,
        ))
    for g in range(groups):
        for j in range(own_blocks):
            mine[g, j, :, pl.ds(0, early)] = scaled(raw, g, j, 0, early)
            twin_mine[g, j] = scaled(twin_raw, g, j, 0, early)
        part = columns(g, my_rep, 0, width)
        near.append(to_core(mine.at[g], part, near_send.at[g], near_recv.at[g], sibling_rep))
        keeps.append(pltpu.make_async_copy(mine.at[g], part, keep_sems.at[g]))
        keeps[-1].start()
        part = columns(g, twin_rep, 0, early)
        near.append(to_core(twin_mine.at[g], part, side_send.at[g], side_recv.at[g], sibling_rep))
        keeps.append(pltpu.make_async_copy(twin_mine.at[g], part, side_keep.at[g]))
        keeps[-1].start()
    passed = []
    for g in range(groups):
        far[g].wait_recv()
        part = columns(g, twin_rep, early, late)
        passed.append(to_core(part, part, pass_send.at[g], pass_recv.at[g], sibling_rep))
    for copy in near + passed:
        copy.wait_recv()
    for copy in keeps:
        copy.wait()
    for copy in sends + twins + [twin_base_copy] + stats + far + near + passed:
        copy.wait_send()


def solution(mesh):
    n_task, n_shard, n_rep = mesh.shape["task"], mesh.shape["shard"], mesh.shape["rep"]

    def shards(deltas, base, sel_index, sel_count, scale_num):
        task_dev, nb_all, rows, width = deltas.shape
        own_blocks, _, groups, _ = base.shape
        layer_tasks = nb_all // LAYERS // own_blocks // n_shard
        dims = (n_task, n_shard, n_rep, layer_tasks)
        peers, group = offset_peers(*dims)
        early = width * EARLY // 8 // LANES * LANES
        hbm = pl.BlockSpec(memory_space=pltpu.HBM)
        return pl.pallas_call(
            functools.partial(kernel, dims),
            out_shape=jax.ShapeDtypeStruct((own_blocks, rows, groups * n_rep * width), jnp.bfloat16),
            in_specs=[hbm] * 5,
            out_specs=pl.BlockSpec(memory_space=pl.ANY),
            scratch_shapes=[
                pltpu.SMEM(sel_index.shape, jnp.int32),
                pltpu.SMEM(sel_count.shape, jnp.int32),
                pltpu.SMEM(scale_num.shape, jnp.int32),
                pltpu.VMEM(deltas.shape, jnp.bfloat16),
                pltpu.VMEM(base.shape, jnp.bfloat16),
                pltpu.VMEM((len(peers), task_dev, rows, width), jnp.bfloat16),
                pltpu.VMEM((len(peers), task_dev, rows, width), jnp.bfloat16),
                pltpu.VMEM((groups, own_blocks, rows, width), jnp.float32),
                pltpu.VMEM((groups, own_blocks, rows, width), jnp.bfloat16),
                pltpu.VMEM((2, LANES), jnp.float32),
                pltpu.VMEM((len(group), 2, LANES), jnp.float32),
                pltpu.VMEM((task_dev, rows, early), jnp.bfloat16),
                pltpu.VMEM((own_blocks, rows, groups, early), jnp.bfloat16),
                pltpu.VMEM((len(peers) + 1, task_dev, rows, early), jnp.bfloat16),
                pltpu.VMEM((groups, own_blocks, rows, early), jnp.float32),
                pltpu.VMEM((groups, own_blocks, rows, early), jnp.bfloat16),
                pltpu.SemaphoreType.DMA((len(peers) + 2,)),
                pltpu.SemaphoreType.DMA((len(peers) + 2,)),
                pltpu.SemaphoreType.DMA((groups,)),
                pltpu.SemaphoreType.DMA((groups,)),
                pltpu.SemaphoreType.DMA((groups,)),
                pltpu.SemaphoreType.DMA((3,)),
                pltpu.SemaphoreType.DMA((task_dev,)),
                pltpu.SemaphoreType.DMA,
                pltpu.SemaphoreType.DMA((len(peers),)),
                pltpu.SemaphoreType.DMA((len(peers),)),
                pltpu.SemaphoreType.DMA((len(group),)),
                pltpu.SemaphoreType.DMA((len(group),)),
                pltpu.SemaphoreType.DMA((groups,)),
                pltpu.SemaphoreType.DMA((groups,)),
                pltpu.SemaphoreType.DMA((groups,)),
                pltpu.SemaphoreType.DMA((groups,)),
                pltpu.SemaphoreType.DMA((groups,)),
                pltpu.SemaphoreType.DMA((groups,)),
                pltpu.SemaphoreType.DMA((groups,)),
            ],
            compiler_params=pltpu.CompilerParams(collective_id=0, has_side_effects=True, vmem_limit_bytes=16 * 1024 * 1024),
        )(*[pltpu.with_memory_space_constraint(x, pltpu.HBM) for x in (sel_index, sel_count, scale_num, deltas, base)])

    placed = (
        P("task", None, None, ("shard", "rep")),
        P(("task", "shard"), None, None, "rep"),
        P(),
        P(),
        P(),
    )
    return jax.shard_map(
        shards,
        mesh=mesh,
        in_specs=placed,
        out_specs=P(("task", "shard"), None, None),
        check_vma=False,
    )
```
